256 devices in a mesh: ctx: 64 (over x, y, z_lo), tp: 4 (over z_hi, core).
Axes of the slice: x: 4, y: 4, z: 8 (z_hi: 2, z_lo: 4; z = z_hi * 4 + z_lo), core: 2. Of those that a mesh axis runs over, the one named last changes fastest.
Arguments:
- span_rows: bfloat16 [2, 2048, 3584], P(None, 'ctx'), may hold values from -6 to 6
- step_rows: bfloat16 [4, 256, 3584], P(None, 'ctx'), may hold values from -6 to 6
- lengths: int32 [2], replicated, may hold values from 4097 to 6144
- sample_prompt: int32 [256], P('ctx'), may hold values from 0 to 1
- norm_gain: float32 [3584], replicated, may hold values from 0.5 to 1.5
- query_weight: bfloat16 [3584, 3584], P('ctx', 'tp'), may hold values from -0.1875 to 0.1875
- key_weight: bfloat16 [3584, 512], P(None, 'tp'), may hold values from -0.1875 to 0.1875
- value_weight: bfloat16 [3584, 512], P(None, 'tp'), may hold values from -0.09375 to 0.09375
- query_bias: float32 [3584], P('tp'), may hold values from -16 to 16
- key_bias: float32 [512], P('tp'), may hold values from -16 to 16
- value_bias: float32 [512], P('tp'), may hold values from -3 to 3
- out_weight: bfloat16 [3584, 3584], P('tp', 'ctx'), may hold values from -0.25 to 0.25
- cache_keys: bfloat16 [2, 4096, 512], P(None, 'ctx', 'tp'), may hold values from -12 to 12
- cache_values: bfloat16 [2, 4096, 512], P(None, 'ctx', 'tp'), may hold values from -6 to 6
Outputs:
- span_out: bfloat16 [2, 2048, 3584], P(None, 'ctx', 'tp')
- dec_out: bfloat16 [4, 256, 3584], P(None, 'ctx', 'tp')
The draws below stay inside these ranges and needn't reach their ends.
All inputs are finite; a program needn't handle non-finite values.
Results may differ from the reference program's by a relative error of at most 0.012.
The reference program's roundings to bfloat16 on the way count: a program that leaves them out, or rounds other values in their place, can miss the bound.
Values may be sent and summed in bfloat16 or wider, within the bound.
A program may use at most 128 MiB of HBM per device.

```python
import math
import jax
import jax.numpy as jnp
from jax import lax

D = 3584
HEADS = 28
KV_HEADS = 4
HEAD = 128
PROMPTS = 2
STEPS = 4
PREFIX = 4096
SPAN = 2048
SAMPLES = 256


def lifted_bias(key, count):
    base = jnp.clip(0.5 * jax.random.normal(key, (count, HEAD), jnp.float32), -3.0, 3.0)
    return base.reshape(count * HEAD)


def draw_query_bias(key, part):
    return lifted_bias(jax.random.fold_in(key, 11), HEADS)


def draw_key_bias(key, part):
    return lifted_bias(jax.random.fold_in(key, 23), KV_HEADS)


def with_ends(drawn, own_key, low, high):
    spot = [jax.random.randint(jax.random.fold_in(own_key, axis), (), 0, length) for axis, length in enumerate(drawn.shape)]
    widest = drawn.shape.index(max(drawn.shape))
    beside = spot[:widest] + [(spot[widest] + 1) % drawn.shape[widest]] + spot[widest + 1:]
    return drawn.at[tuple(spot)].set(low).at[tuple(beside)].set(high)


def steps_of(stream_key, dims, cuts, low, top_value):
    loudness = 1.0
    for axis_at, shards_of in cuts:
        heights = jax.random.uniform(jax.random.fold_in(jax.random.fold_in(stream_key, 6), axis_at), (shards_of,), jnp.float32, low / len(cuts), top_value / len(cuts))
        loudness = loudness * jnp.repeat(jnp.exp(heights), dims[axis_at] // shards_of).reshape((-1,) + (1,) * (len(dims) - 1 - axis_at))
    return loudness


def scatter_about(rng, dims, deviation, limit, shards=(), kind=jnp.bfloat16):
    loudness = steps_of(rng, dims, shards, -0.22, 0.18) if shards else 1.0
    entries = jax.random.normal(rng, dims, jnp.float32) * deviation * loudness
    return jnp.minimum(jnp.maximum(entries, -limit), limit).astype(kind)


def setup_inputs(seed: int = 0) -> dict:
    seeds = jax.random.split(jax.random.key(seed), 15)
    span_rows = scatter_about(seeds[0], (PROMPTS, SPAN, D), 1.0, 6.0, ((1, 64),))
    step_rows = scatter_about(seeds[1], (STEPS, SAMPLES, D), 1.0, 6.0, ((1, 64),))
    lengths = jax.random.randint(seeds[2], (PROMPTS,), PREFIX + 1, PREFIX + SPAN + 1).astype(jnp.int32)
    sample_prompt = with_ends(jax.random.randint(seeds[3], (SAMPLES,), 0, PROMPTS), jax.random.fold_in(seeds[3], 1), 0, PROMPTS - 1).astype(jnp.int32)
    norm_gain = jnp.clip(1.0 + 0.1 * jax.random.normal(seeds[4], (D,), jnp.float32), 0.5, 1.5)
    query_weight = scatter_about(seeds[5], (D, HEADS * HEAD), (D // 4) ** -0.5, 0.1875, ((0, 64), (1, 4)))
    key_weight = scatter_about(seeds[6], (D, KV_HEADS * HEAD), (D // 4) ** -0.5, 0.1875, ((1, 4),))
    value_weight = scatter_about(seeds[7], (D, KV_HEADS * HEAD), D ** -0.5, 0.09375, ((1, 4),))
    query_bias = draw_query_bias(jax.random.fold_in(seeds[14], 71), 0)
    key_bias = draw_key_bias(jax.random.fold_in(seeds[14], 71), 0)
    value_bias = scatter_about(seeds[10], (KV_HEADS * HEAD,), 0.5, 3.0, ((0, 4),), jnp.float32)
    out_weight = scatter_about(seeds[11], (HEADS * HEAD, D), (HEADS * HEAD // 8) ** -0.5, 0.25, ((0, 4), (1, 64)))
    cache_keys = scatter_about(seeds[12], (PROMPTS, PREFIX, KV_HEADS * HEAD), 2.0, 12.0, ((1, 64), (2, 4)))
    cache_values = scatter_about(seeds[13], (PROMPTS, PREFIX, KV_HEADS * HEAD), 1.0, 6.0, ((1, 64), (2, 4)))
    return {"span_rows": span_rows, "step_rows": step_rows, "lengths": lengths, "sample_prompt": sample_prompt, "norm_gain": norm_gain, "query_weight": query_weight, "key_weight": key_weight, "value_weight": value_weight, "query_bias": query_bias, "key_bias": key_bias, "value_bias": value_bias, "out_weight": out_weight, "cache_keys": cache_keys, "cache_values": cache_values}


ROPE_BASE = 1000000.0
NORM_EPS = 1e-06
MASKED = -1e+30

def norm_rows(inputs, norm_gain):
    widened = inputs.astype(jnp.float32)
    inverse = lax.rsqrt(lax.optimization_barrier(jnp.mean(widened * widened, axis=-1, keepdims=True)) + NORM_EPS)
    return (widened * inverse * norm_gain).astype(jnp.bfloat16)

def rotate(vectors, positions):
    width = vectors.shape[-1]
    half = width // 2
    exponent = jnp.arange(half, dtype=jnp.float32) * (2.0 / width)
    frequency = jnp.exp(exponent * -math.log(ROPE_BASE))
    angles = positions.astype(jnp.float32)[..., None, None] * frequency
    cosine = jnp.cos(angles)
    sine = jnp.sin(angles)
    first = vectors[..., :half]
    second = vectors[..., half:]
    return jnp.concatenate([first * cosine - second * sine, second * cosine + first * sine], axis=-1)

def project(normed, weight, bias):
    return jnp.dot(normed, weight, preferred_element_type=jnp.float32) + bias

def attend(query_rows, key_rows, value_rows, visible):
    scores = jnp.dot(query_rows, key_rows.T, preferred_element_type=jnp.float32) * HEAD ** (-0.5)
    scores = jnp.where(visible, scores, MASKED)
    highest = lax.optimization_barrier(jnp.max(scores, axis=-1, keepdims=True))
    weights = jnp.where(visible, jnp.exp(scores - highest), 0.0)
    totals = lax.optimization_barrier(jnp.sum(weights, axis=-1, keepdims=True))
    blended = jnp.dot(weights.astype(jnp.bfloat16), value_rows, preferred_element_type=jnp.float32)
    return (blended / totals).astype(jnp.bfloat16)

def attend_decode(query_rows, key_rows, value_rows, prefix_visible, own_keys, own_values, own_visible):
    factor = HEAD ** (-0.5)
    far_scores = jnp.dot(query_rows, key_rows.T, preferred_element_type=jnp.float32) * factor
    far_scores = jnp.where(prefix_visible, far_scores, MASKED)
    near_scores = jnp.einsum('sd,std->st', query_rows.astype(jnp.float32), own_keys.astype(jnp.float32)) * factor
    near_scores = jnp.where(own_visible[None, :], near_scores, MASKED)
    highest = jnp.maximum(lax.optimization_barrier(jnp.max(far_scores, axis=-1)), lax.optimization_barrier(jnp.max(near_scores, axis=-1)))[:, None]
    far_weights = jnp.where(prefix_visible, jnp.exp(far_scores - highest), 0.0)
    near_weights = jnp.where(own_visible[None, :], jnp.exp(near_scores - highest), 0.0)
    totals = lax.optimization_barrier(jnp.sum(far_weights, axis=-1)) + lax.optimization_barrier(jnp.sum(near_weights, axis=-1))
    near_rounded = lax.optimization_barrier(near_weights.astype(jnp.bfloat16))
    blended = jnp.dot(far_weights.astype(jnp.bfloat16), value_rows, preferred_element_type=jnp.float32)
    blended = blended + jnp.einsum('st,std->sd', near_rounded.astype(jnp.float32), own_values.astype(jnp.float32))
    return (blended / totals[:, None]).astype(jnp.bfloat16)

def reference(span_rows, step_rows, lengths, sample_prompt, norm_gain, query_weight, key_weight, value_weight, query_bias, key_bias, value_bias, out_weight, cache_keys, cache_values):
    kv_group = HEADS // KV_HEADS
    positions_all = PREFIX + SPAN
    normed = norm_rows(span_rows, norm_gain)
    span_places = PREFIX + jnp.arange(SPAN, dtype=jnp.int32)
    grid_places = jnp.broadcast_to(span_places, (PROMPTS, SPAN))
    queries = rotate(project(normed, query_weight, query_bias).reshape(PROMPTS, SPAN, HEADS, HEAD), grid_places).astype(jnp.bfloat16)
    new_keys = rotate(project(normed, key_weight, key_bias).reshape(PROMPTS, SPAN, KV_HEADS, HEAD), grid_places).astype(jnp.bfloat16)
    new_values = project(normed, value_weight, value_bias).astype(jnp.bfloat16).reshape(PROMPTS, SPAN, KV_HEADS, HEAD)
    all_keys = jnp.concatenate([cache_keys.reshape(PROMPTS, PREFIX, KV_HEADS, HEAD), new_keys], axis=1)
    all_values = jnp.concatenate([cache_values.reshape(PROMPTS, PREFIX, KV_HEADS, HEAD), new_values], axis=1)
    key_places = jnp.arange(positions_all, dtype=jnp.int32)
    head_ids = jnp.arange(HEADS, dtype=jnp.int32)
    span_parts = []
    for prompt in range(PROMPTS):
        visible = (key_places[None, :] < lengths[prompt]) & (key_places[None, :] <= span_places[:, None])
        prompt_queries = queries[prompt]
        prompt_keys = all_keys[prompt]
        prompt_values = all_values[prompt]

        def one_head(head_index):
            kv_index = head_index // kv_group
            query_rows = lax.dynamic_index_in_dim(prompt_queries, head_index, 1, keepdims=False)
            key_rows = lax.dynamic_index_in_dim(prompt_keys, kv_index, 1, keepdims=False)
            value_rows = lax.dynamic_index_in_dim(prompt_values, kv_index, 1, keepdims=False)
            return attend(query_rows, key_rows, value_rows, visible)
        per_head = lax.map(one_head, head_ids)
        span_parts.append(jnp.transpose(per_head, (1, 0, 2)).reshape(SPAN, HEADS * HEAD))
    span_attention = jnp.stack(span_parts)
    span_out = jnp.dot(span_attention, out_weight, preferred_element_type=jnp.float32).astype(jnp.bfloat16)
    length_of = lengths[sample_prompt]
    prompt_ids = jnp.arange(PROMPTS, dtype=jnp.int32)
    prefix_visible = ((sample_prompt[:, None, None] == prompt_ids[None, :, None]) & (key_places[None, None, :] < length_of[:, None, None])).reshape(SAMPLES, PROMPTS * positions_all)
    flat_keys = all_keys.reshape(PROMPTS * positions_all, KV_HEADS, HEAD)
    flat_values = all_values.reshape(PROMPTS * positions_all, KV_HEADS, HEAD)
    made_keys = jnp.zeros((SAMPLES, STEPS, KV_HEADS, HEAD), jnp.bfloat16)
    made_values = jnp.zeros((SAMPLES, STEPS, KV_HEADS, HEAD), jnp.bfloat16)
    step_ids = jnp.arange(STEPS, dtype=jnp.int32)
    results = []
    for step_index in range(STEPS):
        normed_step = norm_rows(step_rows[step_index], norm_gain)
        places_now = length_of + step_index
        step_queries = rotate(project(normed_step, query_weight, query_bias).reshape(SAMPLES, HEADS, HEAD), places_now).astype(jnp.bfloat16)
        fresh_keys = rotate(project(normed_step, key_weight, key_bias).reshape(SAMPLES, KV_HEADS, HEAD), places_now).astype(jnp.bfloat16)
        fresh_values = project(normed_step, value_weight, value_bias).astype(jnp.bfloat16).reshape(SAMPLES, KV_HEADS, HEAD)
        made_keys = made_keys.at[:, step_index].set(fresh_keys)
        made_values = made_values.at[:, step_index].set(fresh_values)
        own_visible = step_ids <= step_index
        current_keys = made_keys
        current_values = made_values

        def decode_head(head_index):
            kv_index = head_index // kv_group
            query_rows = lax.dynamic_index_in_dim(step_queries, head_index, 1, keepdims=False)
            key_rows = lax.dynamic_index_in_dim(flat_keys, kv_index, 1, keepdims=False)
            value_rows = lax.dynamic_index_in_dim(flat_values, kv_index, 1, keepdims=False)
            own_keys = lax.dynamic_index_in_dim(current_keys, kv_index, 2, keepdims=False)
            own_values = lax.dynamic_index_in_dim(current_values, kv_index, 2, keepdims=False)
            return attend_decode(query_rows, key_rows, value_rows, prefix_visible, own_keys, own_values, own_visible)
        per_head = lax.map(decode_head, head_ids)
        step_attention = jnp.transpose(per_head, (1, 0, 2)).reshape(SAMPLES, HEADS * HEAD)
        results.append(jnp.dot(step_attention, out_weight, preferred_element_type=jnp.float32).astype(jnp.bfloat16))
    return (span_out, jnp.stack(results))
```

```python
import functools
import math

import jax
import jax.numpy as jnp
from jax import lax
from jax.experimental import pallas as pl
from jax.experimental.pallas import tpu as pltpu
from jax.sharding import PartitionSpec as P

HEADS = 28
KV_HEADS = 4
HEAD = 128


ROPE_BASE = 1000000.0
NORM_EPS = 1e-06
MASKED = -1e30


MESH_ID = pl.DeviceIdType.MESH
RING = 4
SLOTS = 13


def gather_kernel(leads, orders, pairs, *refs):
    count = len(leads)
    blocks, fulls = refs[:count], refs[count : 2 * count]
    local_sem, send_sem, recv_sem = refs[2 * count :]
    me = lax.axis_index("ctx")
    place = {"x": me // 16, "y": lax.rem(me // 4, RING), "z": lax.rem(me, RING)}

    def moved(axis, by):
        there = dict(place)
        there[axis] = lax.rem(place[axis] + by + RING, RING)
        return there

    def device(there):
        return {"ctx": (there["x"] * RING + there["y"]) * RING + there["z"]}

    def part(c, **where):
        index = tuple(where.get(axis, slice(None)) for axis in "xyz")
        return fulls[c].at[(slice(None),) * leads[c] + index]

    def copy(c, slot, source, target, there):
        return pltpu.make_async_remote_copy(
            src_ref=source,
            dst_ref=target,
            send_sem=send_sem.at[c, slot],
            recv_sem=recv_sem.at[c, slot],
            device_id=device(there),
            device_id_type=MESH_ID,
        )

    copies = {}

    def begin(c, slot, source, target, there):
        copies[c, slot] = copy(c, slot, source, target, there)
        copies[c, slot].start()

    def arrived(c, *slots):
        for slot in slots:
            copies[c, slot].wait_recv()

    peers = [moved("z", by) for by in (1, 2, 3)]
    peers += [moved(axis, by) for axis in "xy" for by in (1, -1)]
    barrier = pltpu.get_barrier_semaphore()
    for peer in peers:
        pl.semaphore_signal(barrier, inc=1, device_id=device(peer), device_id_type=MESH_ID)
    pl.semaphore_wait(barrier, len(peers))

    own = []
    for c in range(count):
        mine = part(c, **place)
        for by in (1, 2, 3):
            begin(c, by - 1, blocks[c], mine, moved("z", by))
        kept = pltpu.make_async_copy(blocks[c], mine, local_sem.at[c])
        kept.start()
        own.append(kept)

    low, high = pl.ds(0, 2), pl.ds(2, 2)

    def middle(c):
        axis = orders[c][0]
        own[c].wait()
        arrived(c, 0, 1, 2)
        slab = part(c, x=place["x"], y=place["y"])
        begin(c, 3, slab, slab, moved(axis, 1))
        begin(c, 4, slab, slab, moved(axis, -1))

    def middle_on(c):
        axis = orders[c][0]
        other = "y" if axis == "x" else "x"
        before, after = moved(axis, -1), moved(axis, 1)
        arrived(c, 3)
        slab = part(c, **{axis: before[axis], other: place[other], "z": low})
        begin(c, 5, slab, slab, after)
        arrived(c, 4)
        slab = part(c, **{axis: after[axis], other: place[other], "z": high})
        begin(c, 6, slab, slab, before)

    def last(c):
        inner, axis = orders[c]
        before, after = moved(axis, -1), moved(axis, 1)
        arrived(c, 5, 6)
        first = part(c, **{axis: place[axis], inner: low})
        second = part(c, **{axis: place[axis], inner: high})
        begin(c, 7, first, first, after)
        begin(c, 8, second, second, before)
        begin(c, 9, second, second, after)
        begin(c, 10, first, first, before)

    def last_on(c):
        inner, axis = orders[c]
        before, after = moved(axis, -1), moved(axis, 1)
        arrived(c, 7)
        slab = part(c, **{axis: before[axis], inner: low})
        begin(c, 11, slab, slab, after)
        arrived(c, 8)
        slab = part(c, **{axis: after[axis], inner: high})
        begin(c, 12, slab, slab, before)

    stages = (middle, middle_on, last, last_on)
    for tick in range(2 * len(pairs) + 2):
        for number in range(len(pairs)):
            stage = tick - 2 * number
            if 0 <= stage < 4:
                for c in pairs[number]:
                    stages[stage](c)
    for c in range(count):
        arrived(c, 9, 10, 11, 12)
        for slot in range(SLOTS):
            copies[c, slot].wait_send()


def gather(blocks, leads, orders, pairs):
    count = len(blocks)
    shapes = [
        jax.ShapeDtypeStruct(b.shape[:k] + (RING,) * 3 + b.shape[k:], b.dtype)
        for b, k in zip(blocks, leads)
    ]
    return pl.pallas_call(
        functools.partial(gather_kernel, leads, orders, pairs),
        out_shape=shapes,
        in_specs=[pl.BlockSpec(memory_space=pltpu.VMEM)] * count,
        out_specs=[pl.BlockSpec(memory_space=pl.ANY)] * count,
        scratch_shapes=[
            pltpu.SemaphoreType.DMA((count,)),
            pltpu.SemaphoreType.DMA((count, SLOTS)),
            pltpu.SemaphoreType.DMA((count, SLOTS)),
        ],
        compiler_params=pltpu.CompilerParams(collective_id=0, has_side_effects=True),
    )(*blocks)


def in_blocks(x, dim, length):
    before, after = (x.shape[:dim], x.shape[dim + 1 :])
    return jnp.moveaxis(x.reshape(*before, length, -1, *after), dim, 0)


def sum_at_owner(x, axis, dim):
    parts = in_blocks(x, dim, lax.axis_size(axis))
    arrived = lax.all_to_all(parts, axis, split_axis=0, concat_axis=0, tiled=True)
    return arrived.astype(jnp.float32).sum(axis=0)


def norm_rows(inputs, norm_gain):
    widened = inputs.astype(jnp.float32)
    inverse = lax.rsqrt(jnp.mean(widened * widened, axis=-1, keepdims=True) + NORM_EPS)
    return (widened * inverse * norm_gain).astype(jnp.bfloat16)


def rotate(vectors, positions):
    width = vectors.shape[-1]
    half = width // 2
    exponent = jnp.arange(half, dtype=jnp.float32) * (2.0 / width)
    frequency = jnp.exp(exponent * -math.log(ROPE_BASE))
    angles = positions.astype(jnp.float32)[..., None, None] * frequency
    cosine = jnp.cos(angles)
    sine = jnp.sin(angles)
    first = vectors[..., :half]
    second = vectors[..., half:]
    return jnp.concatenate(
        [first * cosine - second * sine, second * cosine + first * sine], axis=-1
    )


def project(normed, weight, bias):
    return jnp.dot(normed, weight, preferred_element_type=jnp.float32) + bias


def key_positions(count, prefix_dev, span_dev, prefix_all):
    row_index = jnp.arange(count, dtype=jnp.int32)
    device = row_index // (prefix_dev + span_dev)
    offset = row_index % (prefix_dev + span_dev)
    return jnp.where(
        offset < prefix_dev,
        device * prefix_dev + offset,
        prefix_all + device * span_dev + offset - prefix_dev,
    )


def local(
    span_rows,
    step_rows,
    lengths,
    sample_prompt,
    norm_gain,
    query_weight,
    key_weight,
    value_weight,
    query_bias,
    key_bias,
    value_bias,
    out_weight,
    cache_keys,
    cache_values,
):
    cycle_size = lax.axis_size("ctx")
    cycle_place = lax.axis_index("ctx")
    prompt_count = span_rows.shape[0]
    span_dev = span_rows.shape[1]
    prefix_dev = cache_keys.shape[1]
    kv_local = key_weight.shape[1] // HEAD
    kv_group = HEADS // KV_HEADS
    heads_local = kv_local * kv_group
    prefix_all = prefix_dev * cycle_size
    factor = HEAD ** (-0.5)
    cut = 4 * HEAD
    out_turned = out_weight.T
    normed = norm_rows(span_rows, norm_gain)
    span_places = prefix_all + cycle_place * span_dev + jnp.arange(span_dev, dtype=jnp.int32)
    grid_places = jnp.broadcast_to(span_places, (prompt_count, span_dev))
    new_keys = rotate(
        project(normed, key_weight, key_bias).reshape(prompt_count, span_dev, kv_local, HEAD),
        grid_places,
    ).astype(jnp.bfloat16)
    new_values = project(normed, value_weight, value_bias).astype(jnp.bfloat16)
    key_block = jnp.concatenate(
        [cache_keys, new_keys.reshape(prompt_count, span_dev, kv_local * HEAD)], axis=1
    )
    value_block = jnp.concatenate([cache_values, new_values], axis=1)
    blocks = [
        query_weight[:, :cut],
        query_weight[:, cut:],
        key_block,
        value_block,
        out_turned[:, :cut],
        out_turned[:, cut:],
    ]
    first, second = ("y", "x"), ("x", "y")
    query_low, query_high, key_all, value_all, out_low, out_high = gather(
        blocks,
        (0, 0, 1, 1, 0, 0),
        (first, second, first, second, second, first),
        ((0, 1), (2, 3), (4, 5)),
    )
    width = query_weight.shape[0] * cycle_size
    key_all = key_all.reshape(prompt_count, -1, HEAD)
    value_all = value_all.reshape(prompt_count, -1, HEAD)
    query_low, query_high = query_low.reshape(width, -1), query_high.reshape(width, -1)
    out_low, out_high = out_low.reshape(width, -1), out_high.reshape(width, -1)

    def project_query(rows):
        sums = [
            jnp.dot(rows, half, preferred_element_type=jnp.float32)
            for half in (query_low, query_high)
        ]
        return jnp.concatenate(sums, axis=-1) + query_bias

    def project_out(rows):
        halves = ((rows[..., :cut], out_low), (rows[..., cut:], out_high))
        sums = [
            jnp.einsum("...k,nk->...n", part, half, preferred_element_type=jnp.float32)
            for part, half in halves
        ]
        return sums[0] + sums[1]

    queries = rotate(
        project_query(normed).reshape(prompt_count, span_dev, heads_local, HEAD),
        grid_places,
    ).astype(jnp.bfloat16)
    query_rows = (
        queries.reshape(prompt_count, span_dev, kv_local, kv_group, HEAD)
        .transpose(0, 2, 1, 3, 4)
        .reshape(prompt_count, kv_local, span_dev * kv_group, HEAD)
    )
    query_places = jnp.repeat(span_places, kv_group)
    row_count = span_dev * kv_group
    highest = jnp.full((prompt_count, kv_local, row_count), MASKED, jnp.float32)
    count = key_all.shape[1]
    places = key_positions(count, prefix_dev, span_dev, prefix_all)
    key_grid = key_all.reshape(prompt_count, count, kv_local, HEAD)
    value_grid = value_all.reshape(prompt_count, count, kv_local, HEAD)
    scores = (
        jnp.einsum("pgqd,pkgd->pgqk", query_rows, key_grid, preferred_element_type=jnp.float32)
        * factor
    )
    visible = (places[None, None, None, :] < lengths[:, None, None, None]) & (
        places[None, None, None, :] <= query_places[None, None, :, None]
    )
    scores = jnp.where(visible, scores, MASKED)
    raised = jnp.maximum(highest, jnp.max(scores, axis=-1))
    weights = jnp.where(visible, jnp.exp(scores - raised[..., None]), 0.0)
    totals = jnp.sum(weights, axis=-1)
    blended = jnp.einsum(
        "pgqk,pkgd->pgqd",
        weights.astype(jnp.bfloat16),
        value_grid,
        preferred_element_type=jnp.float32,
    )
    highest, totals, blended = (raised, totals, blended)
    span_attention = (blended / totals[..., None]).astype(jnp.bfloat16)
    span_attention = (
        span_attention.reshape(prompt_count, kv_local, span_dev, kv_group, HEAD)
        .transpose(0, 2, 1, 3, 4)
        .reshape(prompt_count, span_dev, heads_local * HEAD)
    )
    span_terms = project_out(span_attention)
    span_out = sum_at_owner(span_terms.astype(jnp.bfloat16), "tp", 2).astype(jnp.bfloat16)
    gathered_rows = key_all.shape[1]
    key_grid = key_all.reshape(prompt_count, gathered_rows, kv_local, HEAD)
    value_grid = value_all.reshape(prompt_count, gathered_rows, kv_local, HEAD)
    all_places = key_positions(gathered_rows, prefix_dev, span_dev, prefix_all)
    picked = sample_prompt[:, None] == jnp.arange(prompt_count, dtype=jnp.int32)[None, :]
    length_of = jnp.sum(jnp.where(picked, lengths[None, :], 0), axis=1)
    prefix_visible = picked[:, :, None] & (all_places[None, None, :] < length_of[:, None, None])
    wide_visible = prefix_visible[:, None, None, :, :]
    sample_count = step_rows.shape[1]
    step_count = step_rows.shape[0]
    step_ids = jnp.arange(step_count, dtype=jnp.int32)
    made_keys = jnp.zeros((sample_count, step_count, kv_local, HEAD), jnp.bfloat16)
    made_values = jnp.zeros((sample_count, step_count, kv_local, HEAD), jnp.bfloat16)
    outputs = []
    for step_index in range(step_count):
        normed_step = norm_rows(step_rows[step_index], norm_gain)
        places_now = length_of + step_index
        step_queries = rotate(
            project_query(normed_step).reshape(sample_count, heads_local, HEAD),
            places_now,
        ).astype(jnp.bfloat16)
        step_queries = step_queries.reshape(sample_count, kv_local, kv_group, HEAD)
        fresh_keys = rotate(
            project(normed_step, key_weight, key_bias).reshape(sample_count, kv_local, HEAD),
            places_now,
        ).astype(jnp.bfloat16)
        fresh_values = (
            project(normed_step, value_weight, value_bias)
            .astype(jnp.bfloat16)
            .reshape(sample_count, kv_local, HEAD)
        )
        made_keys = made_keys.at[:, step_index].set(fresh_keys)
        made_values = made_values.at[:, step_index].set(fresh_values)
        own_visible = step_ids <= step_index
        far_scores = (
            jnp.einsum(
                "sgqd,pkgd->sgqpk", step_queries, key_grid, preferred_element_type=jnp.float32
            )
            * factor
        )
        far_scores = jnp.where(wide_visible, far_scores, MASKED)
        near_scores = (
            jnp.einsum(
                "sgqd,stgd->sgqt", step_queries, made_keys, preferred_element_type=jnp.float32
            )
            * factor
        )
        near_scores = jnp.where(own_visible, near_scores, MASKED)
        highest_now = jnp.maximum(jnp.max(far_scores, axis=(3, 4)), jnp.max(near_scores, axis=-1))
        far_weights = jnp.where(
            wide_visible, jnp.exp(far_scores - highest_now[..., None, None]), 0.0
        )
        near_weights = jnp.where(own_visible, jnp.exp(near_scores - highest_now[..., None]), 0.0)
        totals_now = jnp.sum(far_weights, axis=(3, 4)) + jnp.sum(near_weights, axis=-1)
        blended_now = jnp.einsum(
            "sgqpk,pkgd->sgqd",
            far_weights.astype(jnp.bfloat16),
            value_grid,
            preferred_element_type=jnp.float32,
        )
        blended_now = blended_now + jnp.einsum(
            "sgqt,stgd->sgqd",
            near_weights.astype(jnp.bfloat16),
            made_values,
            preferred_element_type=jnp.float32,
        )
        step_attention = (
            (blended_now / totals_now[..., None])
            .astype(jnp.bfloat16)
            .reshape(sample_count, heads_local * HEAD)
        )
        outputs.append(step_attention)
    stacked = jnp.stack(outputs)
    decode_terms = project_out(stacked)
    dec_out = sum_at_owner(decode_terms.astype(jnp.bfloat16), "tp", 2).astype(jnp.bfloat16)
    return (span_out, dec_out)


def solution(mesh):
    return jax.shard_map(
        local,
        mesh=mesh,
        in_specs=(
            P(None, "ctx", None),
            P(None, "ctx", None),
            P(),
            P("ctx"),
            P(),
            P("ctx", "tp"),
            P(None, "tp"),
            P(None, "tp"),
            P("tp"),
            P("tp"),
            P("tp"),
            P("tp", "ctx"),
            P(None, "ctx", "tp"),
            P(None, "ctx", "tp"),
        ),
        out_specs=(P(None, "ctx", "tp"), P(None, "ctx", "tp")),
        check_vma=False,
    )
```
